32 devices in a mesh: groups: 2 (over x), dev: 16 (over z, y, core).
Axes of the slice: x: 2, y: 2, z: 4, core: 2. Of those that a mesh axis runs over, the one named last changes fastest.
Arguments:
- queries: bfloat16 [2, 32, 128, 1024], P(None, ('groups', 'dev')), parts along dimension 1, may hold values from -180 to 180
- keys_values: bfloat16 [2, 32, 2, 1664, 128], P(None, ('groups', 'dev')), parts along dimension 1, may hold values from -6 to 6
- residual: bfloat16 [2, 2048, 2048], P(None, ('groups', 'dev')), parts along dimension 1, may hold values from -6 to 6
- norm_gain: float32 [2048], replicated, may hold values from 0.1 to 1.9
- gate_up: bfloat16 [16, 2048, 1536], P('dev'), may hold values from -0.125 to 0.125
- down_proj: bfloat16 [16, 768, 2048], P('dev'), may hold values from -0.21875 to 0.21875
- expert_ids: int32 [2, 2048, 8], P(None, ('groups', 'dev')), parts along dimension 1, may hold values from 0 to 15, all different within a row; in each aligned block of 64 rows (0 to 63, 64 to 127, ..., all dimensions but the last counted through in order) at most 40 rows name the same one
- expert_gates: int32 [2, 2048, 8], P(None, ('groups', 'dev')), parts along dimension 1, may hold values from 1 to 1023
Outputs:
- layer_out: bfloat16 [2, 2048, 2048], P(None, ('groups', 'dev')), parts along dimension 1
The draws below stay inside these ranges and needn't reach their ends.
There are 2 independent parts, one for each index of `groups`. The reference program is written for one: setup_inputs(seed, part) draws one part's arguments, and reference() takes and returns one part's arrays. A program takes and returns all parts, laid end to end along the dimension named above; an argument that names none is the same for every part. Nothing has to cross between parts.
Inputs may be any that keep to these rules, and one draw needn't show every extreme that they name: `expert_ids`: in each micro-batch and each aligned block of 64 rows (the tokens of one device), no expert is named by more than 40 rows, a bound that some block reaches; the 8 experts of a row differ.
All inputs are finite; a program needn't handle non-finite values.
Results may differ from the reference program's by a relative error of at most 0.0039.
Values may be sent and summed in bfloat16 or wider, within the bound.
A program may use at most 128 MiB of HBM per device.

```python
import math
import jax
import jax.numpy as jnp
import numpy as np
from jax import lax

D = 2048
FF = 768
HD = 128
GQ = 8
KVH = 2
TOPK = 8
MB = 2
SPAN = 128
SEQS = 8
UNITS = 16
CTX = 1664
TOK_DEV = 64
TOKENS = 1024
EXPERTS = 16
CAP = 40
N_DEV = 16


def joint_draw(key):
    seed_pairs = jax.random.fold_in(key, 101)
    seed_query = jax.random.fold_in(key, 202)
    cached_pairs = jnp.clip(jax.random.normal(seed_pairs, (MB, UNITS, 2, CTX, HD), jnp.float32), -6.0, 6.0)
    query_rows = jnp.clip(2.0 * jax.random.normal(seed_query, (MB, UNITS, SPAN, GQ * HD), jnp.float32), -12.0, 12.0)
    return (cached_pairs, query_rows)


def draw_queries(key, part):
    return joint_draw(key)[1].astype(jnp.bfloat16)


def draw_keys_values(key, part):
    return joint_draw(key)[0].astype(jnp.bfloat16)


def plant(result, key, smallest, top_value):
    longest = result.shape.index(max(result.shape))
    spots = []
    for shift in (0, 1):
        where = [jax.random.randint(jax.random.fold_in(key, axis), (), 0, length) for axis, length in enumerate(result.shape)]
        where[longest] = (where[longest] + shift) % result.shape[longest]
        spots.append(tuple(where))
    return result.at[spots[0]].set(smallest).at[spots[1]].set(top_value)


def block_levels(key, dims, cuts, smallest, high):
    level, own = 1.0, jax.random.fold_in(key, 6)
    for axis_at, parts in cuts:
        draws = jnp.exp(jax.random.uniform(jax.random.fold_in(own, axis_at), (parts,), jnp.float32, smallest / len(cuts), high / len(cuts)))
        level = level * jnp.repeat(draws, dims[axis_at] // parts).reshape([-1 if axis == axis_at else 1 for axis in range(len(dims))])
    return level


def routed_block(key, own, number, rows, number_of, top, most, skew):
    order = jax.random.permutation(key, number_of)
    crowded, ordinary = load_shares(number_of, rows * top, most, skew, True), load_shares(number_of, rows * top, most, skew, False)
    places = jnp.arange(number_of)

    def named(lengths, offset_by):
        used = int((lengths > 0).sum())
        fixed = max(1, used // 4)
        shifted = fixed + (places - fixed + offset_by * (used - fixed)) % max(1, number_of - fixed)
        return jnp.zeros((number_of,), jnp.int32).at[order[jnp.where(places < fixed, places, shifted)]].set(jnp.asarray(lengths, jnp.int32))

    lengths = jnp.where(number % 4 == 0, named(crowded, number // 4), named(ordinary, number - number // 4 - 1))
    mixed = jax.random.permutation(jax.random.fold_in(own, 3), number_of)
    giver, receiver = mixed[0:number_of // 2 * 2:2], mixed[1:number_of // 2 * 2:2]
    slack = jnp.minimum(lengths[giver] - 1, most - lengths[receiver]) // 2
    slack = jnp.where((giver == order[0]) | (receiver == order[0]) | (lengths[receiver] == 0), 0, jnp.maximum(slack, 0))
    shifted = jax.random.randint(jax.random.fold_in(own, 4), (number_of // 2,), 0, 1 << 20) % (slack + 1)
    lengths = lengths.at[giver].add(-shifted).at[receiver].add(shifted)
    labels = jnp.searchsorted(jnp.cumsum(lengths), jnp.arange(rows * top), side="right").astype(jnp.int32)
    table = labels.reshape(top, rows).T
    table = table[jax.random.permutation(jax.random.fold_in(own, 1), rows)]
    offset_by = jax.random.randint(jax.random.fold_in(own, 2), (rows, 1), 0, top)
    return jnp.take_along_axis(table, (jnp.arange(top)[None, :] + offset_by) % top, axis=1)


def load_shares(number_of, total, most, slope, full):
    portions = [(1 << 20) // math.isqrt(rank ** slope) + 1 for rank in range(1, number_of + 1)]
    largest = most if full else min(most, max(-(-total // number_of), total * portions[0] // sum(portions)))
    least = 1 if total - largest >= number_of - 1 else 0
    counts, spare = [largest] + [least] * (number_of - 1), total - largest - least * (number_of - 1)
    while spare > 0:
        free = [i for i in range(1, number_of) if counts[i] < largest] or [i for i in range(1, number_of) if counts[i] < most]
        whole, remaining = sum([portions[i] for i in free]), spare
        for i in free:
            extra = min(most - counts[i], max(1, remaining * portions[i] // whole), spare)
            counts[i] = counts[i] + extra
            spare = spare - extra
    return np.array(counts)


def centred(stream_key, extent, width, limit, shards=(), kind=jnp.bfloat16):
    values = width * jax.random.normal(stream_key, extent, jnp.float32)
    if shards:
        values = values * block_levels(stream_key, extent, shards, -0.22, 0.18)
    return jnp.clip(values, -limit, limit).astype(kind)


def setup_inputs(seed: int = 0, part: int = 0) -> dict:
    streams_of = jax.random.split(jax.random.key(seed), 9)
    part_splits = jax.random.split(jax.random.fold_in(streams_of[8], part), 9)
    queries = draw_queries(jax.random.fold_in(jax.random.fold_in(streams_of[8], part), 71), part)
    keys_values = draw_keys_values(jax.random.fold_in(jax.random.fold_in(streams_of[8], part), 71), part)
    residual = centred(part_splits[2], (MB, TOKENS, D), 1.0, 6.0, ((1, 16),))
    norm_gain = jnp.clip(1.0 + 0.18 * jax.random.normal(streams_of[3], (D,), jnp.float32), 0.1, 1.9)
    gate_up = centred(streams_of[4], (EXPERTS, D, 2 * FF), D ** -0.5, 0.125, ((0, 16),))
    down_proj = centred(streams_of[5], (EXPERTS, FF, D), FF ** -0.5, 0.21875, ((0, 16),))
    expert_ids_keys = jax.random.split(jax.random.fold_in(part_splits[6], 1), MB * TOKENS // TOK_DEV)
    expert_ids_turns = jax.random.permutation(jax.random.fold_in(part_splits[6], 3), MB * TOKENS // TOK_DEV)
    expert_ids = jax.vmap(lambda own, number: routed_block(jax.random.fold_in(part_splits[6], 2), own, number, TOK_DEV, EXPERTS, TOPK, CAP, 1))(expert_ids_keys, expert_ids_turns).reshape((MB, TOKENS, TOPK))
    expert_gates = plant(jax.random.randint(part_splits[7], (MB, TOKENS, TOPK), 1, 1024), jax.random.fold_in(part_splits[7], 1), 1, 1023).astype(jnp.int32)
    return {"queries": queries, "keys_values": keys_values, "residual": residual, "norm_gain": norm_gain, "gate_up": gate_up, "down_proj": down_proj, "expert_ids": expert_ids, "expert_gates": expert_gates}


def attend(query_rows, cached_pairs):
    batches, length, feat_width = query_rows.shape
    context = cached_pairs.shape[2]
    head_size = cached_pairs.shape[3]
    groups = feat_width // head_size
    head_rows = query_rows.reshape(batches, length, groups, head_size).astype(jnp.float32)
    scores = jnp.einsum('mqgd,mkd->mgqk', head_rows, cached_pairs[:, 0].astype(jnp.float32)) / math.sqrt(head_size)
    query_pos = context - length + lax.broadcasted_iota(jnp.int32, (length, context), 0)
    key_pos = lax.broadcasted_iota(jnp.int32, (length, context), 1)
    allowed = key_pos <= query_pos
    scores = jnp.where(allowed, scores, -1e+30)
    highest = lax.optimization_barrier(jnp.max(scores, axis=-1, keepdims=True))
    scaled_exp = jnp.where(allowed, jnp.exp(scores - highest), 0.0)
    totals = lax.optimization_barrier(jnp.sum(scaled_exp, axis=-1, keepdims=True))
    weights = (scaled_exp / totals).astype(jnp.bfloat16)
    blended = jnp.einsum('mgqk,mkd->mqgd', weights.astype(jnp.float32), cached_pairs[:, 1].astype(jnp.float32))
    return blended.astype(jnp.bfloat16).reshape(batches, length, feat_width)

def reference(queries, keys_values, residual, norm_gain, gate_up, down_proj, expert_ids, expert_gates):
    unit_first = (jnp.moveaxis(queries, 1, 0), jnp.moveaxis(keys_values, 1, 0))
    blended_heads = lax.map(lambda unit_pair: attend(unit_pair[0], unit_pair[1]), unit_first)
    grouped = blended_heads.reshape(SEQS, KVH, MB, N_DEV, SPAN // N_DEV, GQ * HD)
    attn_rows = jnp.transpose(grouped, (2, 3, 0, 4, 1, 5)).reshape(MB, TOKENS, D)
    stream = residual.astype(jnp.float32) + attn_rows.astype(jnp.float32)
    meansq = lax.optimization_barrier(jnp.mean(stream * stream, axis=-1, keepdims=True))
    normed = (stream * lax.rsqrt(meansq + 1e-06) * norm_gain).astype(jnp.bfloat16)
    shares = expert_gates.astype(jnp.float32)
    shares = shares / lax.optimization_barrier(jnp.sum(shares, axis=-1, keepdims=True))
    flat_ids = expert_ids.reshape(MB, N_DEV, TOK_DEV * TOPK)
    one_hot = (flat_ids[..., None] == jnp.arange(EXPERTS, dtype=jnp.int32)).astype(jnp.int32)
    ranking = lax.optimization_barrier(jnp.sum((jnp.cumsum(one_hot, axis=2) - one_hot) * one_hot, axis=-1)).astype(jnp.int32)
    batch_ids = lax.broadcasted_iota(jnp.int32, flat_ids.shape, 0)
    source_ids = lax.broadcasted_iota(jnp.int32, flat_ids.shape, 1)
    entry_ids = lax.broadcasted_iota(jnp.int32, flat_ids.shape, 2)
    token_rows = (batch_ids * TOKENS + source_ids * TOK_DEV + entry_ids // TOPK).astype(jnp.int32)
    row_table = jnp.zeros((EXPERTS, MB, N_DEV, CAP), jnp.int32).at[flat_ids, batch_ids, source_ids, ranking].set(token_rows)
    share_table = jnp.zeros((EXPERTS, MB, N_DEV, CAP), jnp.float32).at[flat_ids, batch_ids, source_ids, ranking].set(shares.reshape(MB, N_DEV, TOK_DEV * TOPK))
    flat_normed = normed.reshape(MB * TOKENS, D)

    def expert_turn(running, inputs):
        row_ids, share_ids, gate_mat, down_mat = inputs
        index_list = row_ids.reshape(-1)
        rows_in = flat_normed[index_list]
        projected = jnp.dot(rows_in, gate_mat, preferred_element_type=jnp.float32)
        hidden = (jax.nn.silu(projected[:, :FF]) * projected[:, FF:]).astype(jnp.bfloat16)
        output = jnp.dot(hidden, down_mat, preferred_element_type=jnp.float32).astype(jnp.bfloat16)
        running = running.at[index_list].add(share_ids.reshape(-1, 1) * output.astype(jnp.float32))
        return (running, None)
    start_sum = jnp.zeros((MB * TOKENS, D), jnp.float32)
    mixture, ignored = lax.scan(expert_turn, start_sum, (row_table, share_table, gate_up, down_proj))
    return (stream + mixture.reshape(MB, TOKENS, D)).astype(jnp.bfloat16)
```

```python
import math

import jax
import jax.numpy as jnp
from jax import lax
from jax.sharding import PartitionSpec as P


def attend(query_rows, cached_pairs):
    batches, length, feat_width = query_rows.shape
    context = cached_pairs.shape[2]
    head_size = cached_pairs.shape[3]
    groups = feat_width // head_size
    head_rows = query_rows.reshape(batches, length, groups, head_size)
    scores = jnp.einsum(
        "mqgd,mkd->mgqk", head_rows, cached_pairs[:, 0], preferred_element_type=jnp.float32
    ) / math.sqrt(head_size)
    query_pos = context - length + lax.broadcasted_iota(jnp.int32, (length, context), 0)
    key_pos = lax.broadcasted_iota(jnp.int32, (length, context), 1)
    allowed = key_pos <= query_pos
    scores = jnp.where(allowed, scores, -1e30)
    highest = jnp.max(scores, axis=-1, keepdims=True)
    scaled_exp = jnp.where(allowed, jnp.exp(scores - highest), 0.0)
    totals = jnp.sum(scaled_exp, axis=-1, keepdims=True)
    weights = (scaled_exp / totals).astype(jnp.bfloat16)
    blended = jnp.einsum(
        "mgqk,mkd->mqgd", weights, cached_pairs[:, 1], preferred_element_type=jnp.float32
    )
    return blended.astype(jnp.bfloat16).reshape(batches, length, feat_width)


def to_owners(exchanged, kv_heads):
    batches, sources, positions, feat_width = exchanged.shape
    grouped = exchanged.reshape(batches, sources // kv_heads, kv_heads, positions, feat_width)
    grouped = jnp.transpose(grouped, (0, 1, 3, 2, 4))
    return grouped.reshape(batches, sources // kv_heads * positions, kv_heads * feat_width)


def prepare(attn_rows, residual, norm_gain):
    stream = residual.astype(jnp.float32) + attn_rows.astype(jnp.float32)
    meansq = jnp.mean(stream * stream, axis=-1, keepdims=True)
    normed = (stream * lax.rsqrt(meansq + 1e-06) * norm_gain).astype(jnp.bfloat16)
    return stream, normed


def dense_shares(expert_ids, expert_gates, experts):
    shares = expert_gates.astype(jnp.float32)
    shares = shares / jnp.sum(shares, axis=-1, keepdims=True)
    named = expert_ids[..., None] == jnp.arange(experts, dtype=jnp.int32)
    return jnp.sum(jnp.where(named, shares[..., None], 0.0), axis=-2)


def run_expert(rows_in, gate_up, down_proj, weight):
    hidden_width = down_proj.shape[1]
    projected = jnp.dot(rows_in, gate_up[0], preferred_element_type=jnp.float32)
    hidden = (jax.nn.silu(projected[:, :hidden_width]) * projected[:, hidden_width:]).astype(
        jnp.bfloat16
    )
    output = jnp.dot(hidden, down_proj[0], preferred_element_type=jnp.float32)
    return (output * weight).astype(jnp.bfloat16)


def body(queries, keys_values, residual, norm_gain, gate_up, down_proj, expert_ids, expert_gates):
    devices = lax.axis_size("dev")
    me = lax.axis_index("dev")
    model_width = residual.shape[2]
    kv_heads = model_width // queries.shape[3]
    experts = devices * gate_up.shape[0]
    own_query = queries[:, 0]
    own_pairs = keys_values[:, 0]
    batches, length, feat_width = own_query.shape
    positions = length // devices
    weights = dense_shares(expert_ids, expert_gates, experts)
    weights = lax.all_gather(weights, "dev", axis=1, tiled=True)
    mine = jnp.sum(
        jnp.where(jnp.arange(experts, dtype=jnp.int32) == me, weights, 0.0), axis=-1, keepdims=True
    )
    pieces = []
    for batch_index in range(batches):
        window = slice(batch_index, batch_index + 1)
        blended_heads = attend(own_query[window], own_pairs[window])
        outgoing_rows = blended_heads.reshape(1, devices, positions, feat_width)
        arrived_rows = lax.all_to_all(outgoing_rows, "dev", split_axis=1, concat_axis=1, tiled=True)
        attn_rows = to_owners(arrived_rows, kv_heads)
        stream, normed = prepare(attn_rows[0], residual[batch_index], norm_gain)
        rows_in = lax.all_gather(normed, "dev", axis=0, tiled=True)
        partial = run_expert(rows_in, gate_up, down_proj, mine[batch_index])
        summed = lax.psum_scatter(partial, "dev", scatter_dimension=0, tiled=True)
        pieces.append((stream + summed.astype(jnp.float32)).astype(jnp.bfloat16))
    return jnp.stack(pieces, axis=0)


def solution(mesh):
    in_specs = (
        P(None, ("groups", "dev"), None, None),
        P(None, ("groups", "dev"), None, None, None),
        P(None, ("groups", "dev"), None),
        P(),
        P("dev", None, None),
        P("dev", None, None),
        P(None, ("groups", "dev"), None),
        P(None, ("groups", "dev"), None),
    )
    out_specs = P(None, ("groups", "dev"), None)
    return jax.shard_map(body, mesh=mesh, in_specs=in_specs, out_specs=out_specs, check_vma=False)
```

```python
import functools
import math

import jax
import jax.numpy as jnp
from jax import lax
from jax.experimental import pallas as pl
from jax.experimental.pallas import tpu as pltpu
from jax.sharding import PartitionSpec as P


def attend(query_rows, cached_pairs):
    batches, length, feat_width = query_rows.shape
    context = cached_pairs.shape[2]
    head_size = cached_pairs.shape[3]
    groups = feat_width // head_size
    head_rows = query_rows.reshape(batches, length, groups, head_size)
    scores = jnp.einsum(
        "mqgd,mkd->mgqk", head_rows, cached_pairs[:, 0], preferred_element_type=jnp.float32
    ) / math.sqrt(head_size)
    query_pos = context - length + lax.broadcasted_iota(jnp.int32, (length, context), 0)
    key_pos = lax.broadcasted_iota(jnp.int32, (length, context), 1)
    allowed = key_pos <= query_pos
    scores = jnp.where(allowed, scores, -1e30)
    highest = jnp.max(scores, axis=-1, keepdims=True)
    scaled_exp = jnp.where(allowed, jnp.exp(scores - highest), 0.0)
    totals = jnp.sum(scaled_exp, axis=-1, keepdims=True)
    weights = (scaled_exp / totals).astype(jnp.bfloat16)
    blended = jnp.einsum(
        "mgqk,mkd->mqgd", weights, cached_pairs[:, 1], preferred_element_type=jnp.float32
    )
    return blended.astype(jnp.bfloat16).reshape(batches, length, feat_width)


def to_owners(exchanged, kv_heads):
    batches, sources, positions, feat_width = exchanged.shape
    grouped = exchanged.reshape(batches, sources // kv_heads, kv_heads, positions, feat_width)
    grouped = jnp.transpose(grouped, (0, 1, 3, 2, 4))
    return grouped.reshape(batches, sources // kv_heads * positions, kv_heads * feat_width)


def prepare(attn_rows, residual, norm_gain):
    stream = residual.astype(jnp.float32) + attn_rows.astype(jnp.float32)
    meansq = jnp.mean(stream * stream, axis=-1, keepdims=True)
    normed = (stream * lax.rsqrt(meansq + 1e-06) * norm_gain).astype(jnp.bfloat16)
    return stream, normed


def dense_shares(expert_ids, expert_gates, experts):
    shares = expert_gates.astype(jnp.float32)
    shares = shares / jnp.sum(shares, axis=-1, keepdims=True)
    named = expert_ids[..., None] == jnp.arange(experts, dtype=jnp.int32)
    return jnp.sum(jnp.where(named, shares[..., None], 0.0), axis=-2)


def run_expert(rows_in, gate_up, down_proj, weight):
    hidden_width = down_proj.shape[1]
    projected = jnp.dot(rows_in, gate_up[0], preferred_element_type=jnp.float32)
    hidden = (jax.nn.silu(projected[:, :hidden_width]) * projected[:, hidden_width:]).astype(
        jnp.bfloat16
    )
    output = jnp.dot(hidden, down_proj[0], preferred_element_type=jnp.float32)
    return (output * weight).astype(jnp.bfloat16)


MESH = pl.DeviceIdType.MESH


def moe_kernel(
    chips, x_ref, w_ref, gu_hbm, dn_hbm, out_ref,
    gathered, partial, pairbuf, ringbuf, gu, dn, xs, act,
    load_sem, ag_send, ag_recv, agp_send, agp_recv, rsp_send, rsp_recv, rs_send, rs_recv,
):
    batches, rows, width = x_ref.shape
    hidden = dn.shape[0]
    far = chips // 2
    me = lax.axis_index("dev")
    core = me % 2
    mine = me // 2
    odd = mine % 2
    pos = odd * ((mine + 1) // 2) + (1 - odd) * ((chips - mine // 2) % chips)

    def chip_at(place):
        q = (place + 2 * chips) % chips
        upper = q // (far + 1)
        some = (q + chips - 1) // chips
        return some * ((1 - upper) * (2 * q - 1) + upper * 2 * (chips - q))

    partner = mine * 2 + (1 - core)
    ahead = (chip_at(pos + 1) * 2 + core, chip_at(pos - 1) * 2 + core)
    sign = (1, -1)

    def remote(src, dst, send, recv, target):
        return pltpu.make_async_remote_copy(
            src_ref=src, dst_ref=dst, send_sem=send, recv_sem=recv,
            device_id={"dev": target}, device_id_type=MESH,
        )

    def ag_copy(way, dist, batch, origin, src=None):
        slot = gathered.at[batch, origin, core]
        return remote(
            slot if src is None else src, slot,
            ag_send.at[way, dist - 1, batch], ag_recv.at[way, dist - 1, batch], ahead[way],
        )

    def pair_copy(batch, origin, src=None):
        slot = gathered.at[batch, origin, core]
        return remote(
            slot if src is None else src, slot,
            agp_send.at[batch, origin], agp_recv.at[batch, origin], partner,
        )

    def pair_arrival(batch, origin):
        slot = gathered.at[batch, origin, 1 - core]
        return remote(slot, slot, agp_send.at[batch, origin], agp_recv.at[batch, origin], partner)

    def sum_copy(batch, dest):
        return remote(
            partial.at[batch, dest, 1 - core], pairbuf.at[batch, dest],
            rsp_send.at[batch, dest], rsp_recv.at[batch, dest], partner,
        )

    def rs_copy(way, turn, batch, dest):
        return remote(
            partial.at[batch, dest, core], ringbuf.at[way, turn, batch],
            rs_send.at[way, turn, batch], rs_recv.at[way, turn, batch], ahead[way],
        )

    loads = (
        pltpu.make_async_copy(gu_hbm.at[0], gu, load_sem.at[0]),
        pltpu.make_async_copy(dn_hbm.at[0], dn, load_sem.at[1]),
    )
    for load in loads:
        load.start()

    barrier = pltpu.get_barrier_semaphore()
    for target in (ahead[0], ahead[1], partner):
        pl.semaphore_signal(barrier, inc=1, device_id={"dev": target}, device_id_type=MESH)
    pl.semaphore_wait(barrier, 3)

    for batch in range(batches):
        for way in range(2):
            ag_copy(way, 1, batch, mine, x_ref.at[batch]).start()
    for batch in range(batches):
        pair_copy(batch, mine, x_ref.at[batch]).start()
        gathered[batch, mine, core] = x_ref[batch]
    for load in loads:
        load.wait()

    tile = 256

    def compute(blocks):
        for at, (batch, chip, which) in enumerate(blocks):
            xs[at * rows : (at + 1) * rows, :] = gathered[batch, chip, which]

        @pl.loop(0, hidden // tile)
        def _(j):
            left = pl.ds(pl.multiple_of(j * tile, tile), tile)
            right = pl.ds(pl.multiple_of(hidden + j * tile, tile), tile)
            gate = jnp.dot(xs[...], gu[:, left], preferred_element_type=jnp.float32)
            up = jnp.dot(xs[...], gu[:, right], preferred_element_type=jnp.float32)
            act[:, left] = (gate / (1.0 + jnp.exp(-gate)) * up).astype(jnp.bfloat16)

        @pl.loop(0, width // (2 * tile))
        def _(j):
            cols = pl.ds(pl.multiple_of(j * 2 * tile, 2 * tile), 2 * tile)
            result = jnp.dot(act[...], dn[:, cols], preferred_element_type=jnp.float32)
            for at, (batch, chip, which) in enumerate(blocks):
                share = w_ref[batch, chip, which][:, :1]
                piece = result[at * rows : (at + 1) * rows]
                partial[batch, chip, which, :, cols] = (piece * share).astype(jnp.bfloat16)

    for batch in range(batches):
        pair_arrival(batch, mine).wait_recv()
    compute([(batch, mine, which) for batch in range(batches) for which in range(2)])
    for batch in range(batches):
        sum_copy(batch, mine).start()

    @pl.loop(0, 2 * (far - 1))
    def _(step):
        dist = step // 2 + 1
        batch = step % 2
        origins = (chip_at(pos - dist), chip_at(pos + dist))
        for way in range(2):
            ag_copy(way, dist, batch, origins[way]).wait_recv()

            @pl.when((dist + 1 < far) | (batch == way))
            def _():
                ag_copy(way, dist + 1, batch, origins[way]).start()

            pair_copy(batch, origins[way]).start()
        for way in range(2):
            pair_arrival(batch, origins[way]).wait_recv()
        compute([(batch, origins[way], which) for way in range(2) for which in range(2)])
        for way in range(2):
            sum_copy(batch, origins[way]).start()

    last = chip_at(pos + far)
    for batch in range(batches):
        ag_copy(batch, far, batch, last).wait_recv()
        pair_copy(batch, last).start()
    for batch in range(batches):
        pair_arrival(batch, last).wait_recv()
    compute([(batch, last, which) for batch in range(batches) for which in range(2)])
    for batch in range(batches):
        sum_copy(batch, last).start()

    def gather_sum(batch, dest):
        return partial[batch, dest, core].astype(jnp.float32) + pairbuf[batch, dest].astype(
            jnp.float32
        )

    for batch in range(batches):
        sum_copy(batch, last).wait_recv()
        partial[batch, last, core] = gather_sum(batch, last).astype(jnp.bfloat16)
        rs_copy(batch, 0, batch, last).start()

    for way in range(2):
        dest = chip_at(pos + sign[way] * (far - 1))
        batch = 1 - way
        sum_copy(batch, dest).wait_recv()
        partial[batch, dest, core] = gather_sum(batch, dest).astype(jnp.bfloat16)
        rs_copy(way, 1, batch, dest).start()
    for way in range(2):
        dest = chip_at(pos + sign[way] * (far - 1))
        batch = way
        sum_copy(batch, dest).wait_recv()
        rs_copy(way, 0, batch, dest).wait_recv()
        partial[batch, dest, core] = (
            gather_sum(batch, dest) + ringbuf[way, 0, batch].astype(jnp.float32)
        ).astype(jnp.bfloat16)
        rs_copy(way, 1, batch, dest).start()

    @pl.loop(0, 2 * (far - 2))
    def _(step):
        turn = step // 2 + 2
        for way in range(2):
            batch = (step + 1 + way) % 2
            dest = chip_at(pos + sign[way] * (far - turn))
            sum_copy(batch, dest).wait_recv()
            rs_copy(way, turn - 1, batch, dest).wait_recv()
            partial[batch, dest, core] = (
                gather_sum(batch, dest) + ringbuf[way, turn - 1, batch].astype(jnp.float32)
            ).astype(jnp.bfloat16)
            rs_copy(way, turn, batch, dest).start()

    for batch in range(batches):
        sum_copy(batch, mine).wait_recv()
    for way in range(2):
        rs_copy(way, far - 1, 1 - way, mine).wait_recv()
    for way in range(2):
        rs_copy(way, far - 1, way, mine).wait_recv()
    for batch in range(batches):
        out_ref[batch] = (
            gather_sum(batch, mine)
            + ringbuf[0, far - 1, batch].astype(jnp.float32)
            + ringbuf[1, far - 1, batch].astype(jnp.float32)
        )

    for way in range(2):
        for batch in range(batches):
            ag_copy(way, 1, batch, mine, x_ref.at[batch]).wait_send()
        ag_copy(way, far, way, mine).wait_send()

        @pl.loop(0, 2 * (far - 2))
        def _(step):
            ag_copy(way, step // 2 + 2, step % 2, mine).wait_send()

        rs_copy(way, 0, way, mine).wait_send()

        @pl.loop(0, 2 * (far - 1))
        def _(step):
            rs_copy(way, step // 2 + 1, step % 2, mine).wait_send()

    @pl.loop(0, 2 * chips)
    def _(step):
        pair_copy(step % 2, step // 2).wait_send()
        sum_copy(step % 2, step // 2).wait_send()


def fits(devices, rows, width, hidden):
    block = 2 * rows * width * 2
    needed = devices * block * 2 + devices // 2 * block + devices // 2 * block
    needed += 3 * width * hidden * 2 + 4 * rows * width * 2 + devices * rows * 2 * 512
    return devices % 4 == 0 and devices >= 8 and needed < 46 * 1024 * 1024


def routed_experts(normed, weights, gate_up, down_proj, devices):
    batches, rows, width = normed.shape
    hidden = down_proj.shape[1]
    chips = devices // 2
    far = chips // 2
    dma = pltpu.SemaphoreType.DMA
    spread = jnp.broadcast_to(
        weights.reshape(batches, chips, 2, rows, 1), (batches, chips, 2, rows, 128)
    )
    vmem = pl.BlockSpec(memory_space=pltpu.VMEM)
    anywhere = pl.BlockSpec(memory_space=pl.ANY)
    kind = jnp.bfloat16
    return pl.pallas_call(
        functools.partial(moe_kernel, chips),
        out_shape=jax.ShapeDtypeStruct((batches, rows, width), jnp.float32),
        in_specs=[vmem, vmem, anywhere, anywhere],
        out_specs=vmem,
        scratch_shapes=[
            pltpu.VMEM((batches, chips, 2, rows, width), kind),
            pltpu.VMEM((batches, chips, 2, rows, width), kind),
            pltpu.VMEM((batches, chips, rows, width), kind),
            pltpu.VMEM((2, far, batches, rows, width), kind),
            pltpu.VMEM((width, 2 * hidden), kind),
            pltpu.VMEM((hidden, width), kind),
            pltpu.VMEM((4 * rows, width), kind),
            pltpu.VMEM((4 * rows, hidden), kind),
            dma((2,)),
            dma((2, far, batches)), dma((2, far, batches)),
            dma((batches, chips)), dma((batches, chips)),
            dma((batches, chips)), dma((batches, chips)),
            dma((2, far, batches)), dma((2, far, batches)),
        ],
        compiler_params=pltpu.CompilerParams(
            collective_id=0, has_side_effects=True, vmem_limit_bytes=56 * 1024 * 1024
        ),
    )(normed, spread, gate_up, down_proj)


def body(queries, keys_values, residual, norm_gain, gate_up, down_proj, expert_ids, expert_gates):
    devices = lax.axis_size("dev")
    me = lax.axis_index("dev")
    model_width = residual.shape[2]
    kv_heads = model_width // queries.shape[3]
    experts = devices * gate_up.shape[0]
    own_query = queries[:, 0]
    own_pairs = keys_values[:, 0]
    batches, length, feat_width = own_query.shape
    positions = length // devices
    weights = dense_shares(expert_ids, expert_gates, experts)
    weights = lax.all_gather(weights, "dev", axis=1, tiled=True)
    mine = jnp.sum(
        jnp.where(jnp.arange(experts, dtype=jnp.int32) == me, weights, 0.0), axis=-1, keepdims=True
    )
    streams, rows_out = [], []
    for batch_index in range(batches):
        window = slice(batch_index, batch_index + 1)
        blended_heads = attend(own_query[window], own_pairs[window])
        outgoing_rows = blended_heads.reshape(1, devices, positions, feat_width)
        arrived_rows = lax.all_to_all(outgoing_rows, "dev", split_axis=1, concat_axis=1, tiled=True)
        attn_rows = to_owners(arrived_rows, kv_heads)
        stream, normed = prepare(attn_rows[0], residual[batch_index], norm_gain)
        streams.append(stream)
        rows_out.append(normed)
    if batches == 2 and fits(devices, residual.shape[1], model_width, down_proj.shape[1]):
        summed = routed_experts(jnp.stack(rows_out), mine, gate_up, down_proj, devices)
        return (jnp.stack(streams) + summed).astype(jnp.bfloat16)
    pieces = []
    for batch_index in range(batches):
        rows_in = lax.all_gather(rows_out[batch_index], "dev", axis=0, tiled=True)
        partial = run_expert(rows_in, gate_up, down_proj, mine[batch_index])
        summed = lax.psum_scatter(partial, "dev", scatter_dimension=0, tiled=True)
        pieces.append((streams[batch_index] + summed.astype(jnp.float32)).astype(jnp.bfloat16))
    return jnp.stack(pieces, axis=0)


def solution(mesh):
    in_specs = (
        P(None, ("groups", "dev"), None, None),
        P(None, ("groups", "dev"), None, None, None),
        P(None, ("groups", "dev"), None),
        P(),
        P("dev", None, None),
        P("dev", None, None),
        P(None, ("groups", "dev"), None),
        P(None, ("groups", "dev"), None),
    )
    out_specs = P(None, ("groups", "dev"), None)
    return jax.shard_map(body, mesh=mesh, in_specs=in_specs, out_specs=out_specs, check_vma=False)
```

```python
import functools
import math

import jax
import jax.numpy as jnp
from jax import lax
from jax.experimental import pallas as pl
from jax.experimental.pallas import tpu as pltpu
from jax.sharding import PartitionSpec as P


def attend(query_rows, cached_pairs):
    batches, length, feat_width = query_rows.shape
    context = cached_pairs.shape[2]
    head_size = cached_pairs.shape[3]
    groups = feat_width // head_size
    head_rows = query_rows.reshape(batches, length, groups, head_size)
    scores = jnp.einsum(
        "mqgd,mkd->mgqk", head_rows, cached_pairs[:, 0], preferred_element_type=jnp.float32
    ) / math.sqrt(head_size)
    query_pos = context - length + lax.broadcasted_iota(jnp.int32, (length, context), 0)
    key_pos = lax.broadcasted_iota(jnp.int32, (length, context), 1)
    allowed = key_pos <= query_pos
    scores = jnp.where(allowed, scores, -1e30)
    highest = jnp.max(scores, axis=-1, keepdims=True)
    scaled_exp = jnp.where(allowed, jnp.exp(scores - highest), 0.0)
    totals = jnp.sum(scaled_exp, axis=-1, keepdims=True)
    weights = (scaled_exp / totals).astype(jnp.bfloat16)
    blended = jnp.einsum(
        "mgqk,mkd->mqgd", weights, cached_pairs[:, 1], preferred_element_type=jnp.float32
    )
    return blended.astype(jnp.bfloat16).reshape(batches, length, feat_width)


def to_owners(exchanged, kv_heads):
    batches, sources, positions, feat_width = exchanged.shape
    grouped = exchanged.reshape(batches, sources // kv_heads, kv_heads, positions, feat_width)
    grouped = jnp.transpose(grouped, (0, 1, 3, 2, 4))
    return grouped.reshape(batches, sources // kv_heads * positions, kv_heads * feat_width)


def prepare(attn_rows, residual, norm_gain):
    stream = residual.astype(jnp.float32) + attn_rows.astype(jnp.float32)
    meansq = jnp.mean(stream * stream, axis=-1, keepdims=True)
    normed = (stream * lax.rsqrt(meansq + 1e-06) * norm_gain).astype(jnp.bfloat16)
    return stream, normed


def dense_shares(expert_ids, expert_gates, experts):
    shares = expert_gates.astype(jnp.float32)
    shares = shares / jnp.sum(shares, axis=-1, keepdims=True)
    named = expert_ids[..., None] == jnp.arange(experts, dtype=jnp.int32)
    return jnp.sum(jnp.where(named, shares[..., None], 0.0), axis=-2)


def run_expert(rows_in, gate_up, down_proj, weight):
    hidden_width = down_proj.shape[1]
    projected = jnp.dot(rows_in, gate_up[0], preferred_element_type=jnp.float32)
    hidden = (jax.nn.silu(projected[:, :hidden_width]) * projected[:, hidden_width:]).astype(
        jnp.bfloat16
    )
    output = jnp.dot(hidden, down_proj[0], preferred_element_type=jnp.float32)
    return (output * weight).astype(jnp.bfloat16)


MESH = pl.DeviceIdType.MESH


def moe_kernel(
    chips, heads_ref, res_ref, gain_ref, share_ref, gu_hbm, dn_hbm, out_ref,
    attn, stream, gathered, partial, pairbuf, ringbuf, gu, dn, xs, sh, act,
    load_sem, ex_send, ex_recv, ag_send, ag_recv, agp_send, agp_recv, rsp_send, rsp_recv, rs_send, rs_recv,
):
    batches, rows, width = res_ref.shape
    devices = 2 * chips
    kv_heads, part = attn.shape[2], attn.shape[4]
    hidden = dn.shape[0]
    far = chips // 2
    me = lax.axis_index("dev")
    core = me % 2
    mine = me // 2
    odd = mine % 2
    pos = odd * ((mine + 1) // 2) + (1 - odd) * ((chips - mine // 2) % chips)

    def chip_at(place):
        q = (place + 2 * chips) % chips
        upper = q // (far + 1)
        some = (q + chips - 1) // chips
        return some * ((1 - upper) * (2 * q - 1) + upper * 2 * (chips - q))

    partner = mine * 2 + (1 - core)
    ahead = (chip_at(pos + 1) * 2 + core, chip_at(pos - 1) * 2 + core)
    sign = (1, -1)

    def remote(src, dst, send, recv, target):
        return pltpu.make_async_remote_copy(
            src_ref=src, dst_ref=dst, send_sem=send, recv_sem=recv,
            device_id={"dev": target}, device_id_type=MESH,
        )

    def ag_copy(way, dist, batch, origin):
        slot = gathered.at[batch, origin, core]
        return remote(
            slot, slot,
            ag_send.at[way, dist - 1, batch], ag_recv.at[way, dist - 1, batch], ahead[way],
        )

    def pair_copy(batch, origin):
        slot = gathered.at[batch, origin, core]
        return remote(slot, slot, agp_send.at[batch, origin], agp_recv.at[batch, origin], partner)

    def pair_arrival(batch, origin):
        slot = gathered.at[batch, origin, 1 - core]
        return remote(slot, slot, agp_send.at[batch, origin], agp_recv.at[batch, origin], partner)

    def sum_copy(batch, dest):
        return remote(
            partial.at[batch, dest, 1 - core], pairbuf.at[batch, dest],
            rsp_send.at[batch, dest], rsp_recv.at[batch, dest], partner,
        )

    def rs_copy(way, turn, batch, dest):
        return remote(
            partial.at[batch, dest, core], ringbuf.at[way, turn, batch],
            rs_send.at[way, turn, batch], rs_recv.at[way, turn, batch], ahead[way],
        )

    def exchange(batch, target):
        return remote(
            heads_ref.at[batch, target], attn.at[batch, me // kv_heads, me % kv_heads],
            ex_send.at[batch, target], ex_recv.at[batch, me], target,
        )

    def arrival(batch, source):
        slot = attn.at[batch, source // kv_heads, source % kv_heads]
        return remote(slot, slot, ex_send.at[batch, source], ex_recv.at[batch, source], source)

    loads = (
        pltpu.make_async_copy(gu_hbm.at[0], gu, load_sem.at[0]),
        pltpu.make_async_copy(dn_hbm.at[0], dn, load_sem.at[1]),
    )
    for load in loads:
        load.start()

    barrier = pltpu.get_barrier_semaphore()

    @pl.loop(1, devices)
    def _(k):
        target = (me + k) % devices
        pl.semaphore_signal(barrier, inc=1, device_id={"dev": target}, device_id_type=MESH)

    pl.semaphore_wait(barrier, devices - 1)

    for batch in range(batches):

        @pl.loop(1, devices)
        def _(k):
            exchange(batch, (me + k) % devices).start()

    for batch in range(batches):
        attn[batch, me // kv_heads, me % kv_heads] = heads_ref[batch, me]
        gathered[batch, mine, core, :, width:] = share_ref[batch]

        @pl.loop(1, devices)
        def _(k):
            arrival(batch, (me + k) % devices).wait_recv()

        squares = jnp.zeros((rows, 1), jnp.float32)
        for head in range(kv_heads):
            cols = slice(head * part, (head + 1) * part)
            added = attn[batch, :, head].astype(jnp.float32).reshape(rows, part)
            added = added + res_ref[batch, :, cols].astype(jnp.float32)
            stream[batch, :, cols] = added
            squares = squares + jnp.sum(added * added, axis=-1, keepdims=True)
        scale = lax.rsqrt(squares / width + 1e-06)
        gathered[batch, mine, core, :, :width] = (
            stream[batch] * scale * gain_ref[...]
        ).astype(jnp.bfloat16)
        for way in range(2):
            ag_copy(way, 1, batch, mine).start()
        pair_copy(batch, mine).start()
    for load in loads:
        load.wait()

    tile = 256

    def compute(blocks):
        for at, (batch, chip, which) in enumerate(blocks):
            xs[at * rows : (at + 1) * rows, :] = gathered[batch, chip, which, :, :width]
            lanes = gathered[batch, chip, which, :, width:].astype(jnp.float32)
            lane = lax.broadcasted_iota(jnp.int32, lanes.shape, 1)
            mask = (lane == me) | (lane == me + devices)
            share = jnp.sum(jnp.where(mask, lanes, 0.0), axis=-1, keepdims=True)
            sh[at * rows : (at + 1) * rows, :] = jnp.broadcast_to(share, lanes.shape)

        @pl.loop(0, hidden // tile)
        def _(j):
            left = pl.ds(pl.multiple_of(j * tile, tile), tile)
            right = pl.ds(pl.multiple_of(hidden + j * tile, tile), tile)
            gate = jnp.dot(xs[...], gu[:, left], preferred_element_type=jnp.float32)
            up = jnp.dot(xs[...], gu[:, right], preferred_element_type=jnp.float32)
            act[:, left] = (gate / (1.0 + jnp.exp(-gate)) * up).astype(jnp.bfloat16)

        @pl.loop(0, width // (2 * tile))
        def _(j):
            cols = pl.ds(pl.multiple_of(j * 2 * tile, 2 * tile), 2 * tile)
            result = jnp.dot(act[...], dn[:, cols], preferred_element_type=jnp.float32)
            for at, (batch, chip, which) in enumerate(blocks):
                share = sh[at * rows : (at + 1) * rows, :1]
                piece = result[at * rows : (at + 1) * rows]
                partial[batch, chip, which, :, cols] = (piece * share).astype(jnp.bfloat16)

    for batch in range(batches):
        pair_arrival(batch, mine).wait_recv()
    compute([(batch, mine, which) for batch in range(batches) for which in range(2)])
    for batch in range(batches):
        sum_copy(batch, mine).start()

    @pl.loop(0, 2 * (far - 1))
    def _(step):
        dist = step // 2 + 1
        batch = step % 2
        origins = (chip_at(pos - dist), chip_at(pos + dist))
        for way in range(2):
            ag_copy(way, dist, batch, origins[way]).wait_recv()

            @pl.when((dist + 1 < far) | (batch == way))
            def _():
                ag_copy(way, dist + 1, batch, origins[way]).start()

            pair_copy(batch, origins[way]).start()
        for way in range(2):
            pair_arrival(batch, origins[way]).wait_recv()
        compute([(batch, origins[way], which) for way in range(2) for which in range(2)])
        for way in range(2):
            sum_copy(batch, origins[way]).start()

    last = chip_at(pos + far)
    for batch in range(batches):
        ag_copy(batch, far, batch, last).wait_recv()
        pair_copy(batch, last).start()
    for batch in range(batches):
        pair_arrival(batch, last).wait_recv()
    compute([(batch, last, which) for batch in range(batches) for which in range(2)])
    for batch in range(batches):
        sum_copy(batch, last).start()

    def gather_sum(batch, dest):
        return partial[batch, dest, core].astype(jnp.float32) + pairbuf[batch, dest].astype(
            jnp.float32
        )

    for batch in range(batches):
        sum_copy(batch, last).wait_recv()
        partial[batch, last, core] = gather_sum(batch, last).astype(jnp.bfloat16)
        rs_copy(batch, 0, batch, last).start()

    for way in range(2):
        dest = chip_at(pos + sign[way] * (far - 1))
        batch = 1 - way
        sum_copy(batch, dest).wait_recv()
        partial[batch, dest, core] = gather_sum(batch, dest).astype(jnp.bfloat16)
        rs_copy(way, 1, batch, dest).start()
    for way in range(2):
        dest = chip_at(pos + sign[way] * (far - 1))
        batch = way
        sum_copy(batch, dest).wait_recv()
        rs_copy(way, 0, batch, dest).wait_recv()
        partial[batch, dest, core] = (
            gather_sum(batch, dest) + ringbuf[way, 0, batch].astype(jnp.float32)
        ).astype(jnp.bfloat16)
        rs_copy(way, 1, batch, dest).start()

    @pl.loop(0, 2 * (far - 2))
    def _(step):
        turn = step // 2 + 2
        for way in range(2):
            batch = (step + 1 + way) % 2
            dest = chip_at(pos + sign[way] * (far - turn))
            sum_copy(batch, dest).wait_recv()
            rs_copy(way, turn - 1, batch, dest).wait_recv()
            partial[batch, dest, core] = (
                gather_sum(batch, dest) + ringbuf[way, turn - 1, batch].astype(jnp.float32)
            ).astype(jnp.bfloat16)
            rs_copy(way, turn, batch, dest).start()

    for batch in range(batches):
        sum_copy(batch, mine).wait_recv()
    for way in range(2):
        rs_copy(way, far - 1, 1 - way, mine).wait_recv()
    for way in range(2):
        rs_copy(way, far - 1, way, mine).wait_recv()
    for batch in range(batches):
        out_ref[batch] = (
            stream[batch]
            + (
                gather_sum(batch, mine)
                + ringbuf[0, far - 1, batch].astype(jnp.float32)
                + ringbuf[1, far - 1, batch].astype(jnp.float32)
            )
        ).astype(out_ref.dtype)

    @pl.loop(1, devices)
    def _(k):
        for batch in range(batches):
            exchange(batch, (me + k) % devices).wait_send()

    for way in range(2):
        for batch in range(batches):
            ag_copy(way, 1, batch, mine).wait_send()
        ag_copy(way, far, way, mine).wait_send()

        @pl.loop(0, 2 * (far - 2))
        def _(step):
            ag_copy(way, step // 2 + 2, step % 2, mine).wait_send()

        rs_copy(way, 0, way, mine).wait_send()

        @pl.loop(0, 2 * (far - 1))
        def _(step):
            rs_copy(way, step // 2 + 1, step % 2, mine).wait_send()

    @pl.loop(0, 2 * chips)
    def _(step):
        pair_copy(step % 2, step // 2).wait_send()
        sum_copy(step % 2, step // 2).wait_send()


def fits(devices, rows, width, hidden):
    block = 2 * rows * (width + 128) * 2
    needed = 3 * devices * block + 3 * width * hidden * 2 + 8 * rows * width * 4
    return devices % 4 == 0 and 8 <= devices <= 64 and needed < 48 * 1024 * 1024


def share_lanes(weights):
    coarse = lax.reduce_precision(weights, 8, 7)
    fine = lax.reduce_precision(weights - coarse, 8, 7)
    both = jnp.concatenate([coarse, fine], axis=-1)
    gap = 128 - both.shape[-1]
    return jnp.pad(both, ((0, 0), (0, 0), (0, gap))).astype(jnp.bfloat16)


def routed_layer(heads, residual, norm_gain, lanes, gate_up, down_proj, kv_heads):
    batches, rows, width = residual.shape
    devices, span, part = heads.shape[1:]
    hidden = down_proj.shape[1]
    chips = devices // 2
    far = chips // 2
    dma = pltpu.SemaphoreType.DMA
    vmem = pl.BlockSpec(memory_space=pltpu.VMEM)
    anywhere = pl.BlockSpec(memory_space=pl.ANY)
    kind = jnp.bfloat16
    return pl.pallas_call(
        functools.partial(moe_kernel, chips),
        out_shape=jax.ShapeDtypeStruct((batches, rows, width), kind),
        in_specs=[vmem, vmem, vmem, vmem, anywhere, anywhere],
        out_specs=vmem,
        scratch_shapes=[
            pltpu.VMEM((batches, devices // kv_heads, kv_heads, span, part), kind),
            pltpu.VMEM((batches, rows, width), jnp.float32),
            pltpu.VMEM((batches, chips, 2, rows, width + 128), kind),
            pltpu.VMEM((batches, chips, 2, rows, width), kind),
            pltpu.VMEM((batches, chips, rows, width), kind),
            pltpu.VMEM((2, far, batches, rows, width), kind),
            pltpu.VMEM((width, 2 * hidden), kind),
            pltpu.VMEM((hidden, width), kind),
            pltpu.VMEM((4 * rows, width), kind),
            pltpu.VMEM((4 * rows, 128), jnp.float32),
            pltpu.VMEM((4 * rows, hidden), kind),
            dma((2,)),
            dma((batches, devices)), dma((batches, devices)),
            dma((2, far, batches)), dma((2, far, batches)),
            dma((batches, chips)), dma((batches, chips)),
            dma((batches, chips)), dma((batches, chips)),
            dma((2, far, batches)), dma((2, far, batches)),
        ],
        compiler_params=pltpu.CompilerParams(
            collective_id=0, has_side_effects=True, vmem_limit_bytes=56 * 1024 * 1024
        ),
    )(heads, residual, norm_gain.reshape(1, width), lanes, gate_up, down_proj)


def body(queries, keys_values, residual, norm_gain, gate_up, down_proj, expert_ids, expert_gates):
    devices = lax.axis_size("dev")
    me = lax.axis_index("dev")
    model_width = residual.shape[2]
    kv_heads = model_width // queries.shape[3]
    experts = devices * gate_up.shape[0]
    own_query = queries[:, 0]
    own_pairs = keys_values[:, 0]
    batches, length, feat_width = own_query.shape
    positions = length // devices
    weights = dense_shares(expert_ids, expert_gates, experts)
    blended = [
        attend(own_query[index : index + 1], own_pairs[index : index + 1])
        for index in range(batches)
    ]
    if batches == 2 and fits(devices, residual.shape[1], model_width, down_proj.shape[1]):
        heads = jnp.concatenate(blended).reshape(batches, devices, positions, feat_width)
        lanes = share_lanes(weights)
        return routed_layer(heads, residual, norm_gain, lanes, gate_up, down_proj, kv_heads)
    weights = lax.all_gather(weights, "dev", axis=1, tiled=True)
    mine = jnp.sum(
        jnp.where(jnp.arange(experts, dtype=jnp.int32) == me, weights, 0.0), axis=-1, keepdims=True
    )
    pieces = []
    for batch_index in range(batches):
        outgoing_rows = blended[batch_index].reshape(1, devices, positions, feat_width)
        arrived_rows = lax.all_to_all(outgoing_rows, "dev", split_axis=1, concat_axis=1, tiled=True)
        attn_rows = to_owners(arrived_rows, kv_heads)
        stream, normed = prepare(attn_rows[0], residual[batch_index], norm_gain)
        rows_in = lax.all_gather(normed, "dev", axis=0, tiled=True)
        partial = run_expert(rows_in, gate_up, down_proj, mine[batch_index])
        summed = lax.psum_scatter(partial, "dev", scatter_dimension=0, tiled=True)
        pieces.append((stream + summed.astype(jnp.float32)).astype(jnp.bfloat16))
    return jnp.stack(pieces, axis=0)


def solution(mesh):
    in_specs = (
        P(None, ("groups", "dev"), None, None),
        P(None, ("groups", "dev"), None, None, None),
        P(None, ("groups", "dev"), None),
        P(),
        P("dev", None, None),
        P("dev", None, None),
        P(None, ("groups", "dev"), None),
        P(None, ("groups", "dev"), None),
    )
    out_specs = P(None, ("groups", "dev"), None)
    return jax.shard_map(body, mesh=mesh, in_specs=in_specs, out_specs=out_specs, check_vma=False)
```

```python
import functools
import math

import jax
import jax.numpy as jnp
from jax import lax
from jax.experimental import pallas as pl
from jax.experimental.pallas import tpu as pltpu
from jax.sharding import PartitionSpec as P


def attend_kernel(heads, q_ref, kv_ref, out_ref):
    length = q_ref.shape[1]
    context, head_size = kv_ref.shape[3:]
    past = context - length
    keys = kv_ref[0, 0, 0]
    query = jnp.concatenate(
        [q_ref[0, :, head * head_size : (head + 1) * head_size] for head in range(heads)], axis=0
    )
    scores = lax.dot_general(
        query, keys, (((1,), (1,)), ((), ())), preferred_element_type=jnp.float32
    )
    scores = scores * (1.0 / math.sqrt(head_size))
    old, new = scores[:, :past], scores[:, past:]
    row = lax.broadcasted_iota(jnp.int32, new.shape, 0) % length
    col = lax.broadcasted_iota(jnp.int32, new.shape, 1)
    allowed = col <= row
    new = jnp.where(allowed, new, -1e30)
    highest = jnp.maximum(
        jnp.max(old, axis=-1, keepdims=True), jnp.max(new, axis=-1, keepdims=True)
    )
    old = jnp.exp(old - highest)
    new = jnp.where(allowed, jnp.exp(new - highest), 0.0)
    totals = jnp.sum(old, axis=-1, keepdims=True) + jnp.sum(new, axis=-1, keepdims=True)
    share = 1.0 / totals
    blended = jnp.dot(
        (old * share).astype(jnp.bfloat16), kv_ref[0, 0, 1, :past, :],
        preferred_element_type=jnp.float32,
    ) + jnp.dot(
        (new * share).astype(jnp.bfloat16), kv_ref[0, 0, 1, past:, :],
        preferred_element_type=jnp.float32,
    )
    for head in range(heads):
        out_ref[0, :, head * head_size : (head + 1) * head_size] = blended[
            head * length : (head + 1) * length
        ].astype(jnp.bfloat16)


def attend_local(queries, keys_values):
    batches, unit, length, feat_width = queries.shape
    context, head_size = keys_values.shape[3:]
    heads = 2
    wide = heads * head_size
    return pl.pallas_call(
        functools.partial(attend_kernel, heads),
        grid=(batches, feat_width // wide),
        out_shape=jax.ShapeDtypeStruct((batches, length, feat_width), jnp.bfloat16),
        in_specs=[
            pl.BlockSpec((1, length, wide), lambda b, h: (b, 0, h)),
            pl.BlockSpec((1, 1, 2, context, head_size), lambda b, h: (b, 0, 0, 0, 0)),
        ],
        out_specs=pl.BlockSpec((1, length, wide), lambda b, h: (b, 0, h)),
        compiler_params=pltpu.CompilerParams(vmem_limit_bytes=40 * 1024 * 1024),
    )(queries.reshape(batches, length, feat_width), keys_values)


def to_owners(exchanged, kv_heads):
    batches, sources, positions, feat_width = exchanged.shape
    grouped = exchanged.reshape(batches, sources // kv_heads, kv_heads, positions, feat_width)
    grouped = jnp.transpose(grouped, (0, 1, 3, 2, 4))
    return grouped.reshape(batches, sources // kv_heads * positions, kv_heads * feat_width)


def prepare(attn_rows, residual, norm_gain):
    stream = residual.astype(jnp.float32) + attn_rows.astype(jnp.float32)
    meansq = jnp.mean(stream * stream, axis=-1, keepdims=True)
    normed = (stream * lax.rsqrt(meansq + 1e-06) * norm_gain).astype(jnp.bfloat16)
    return stream, normed


def dense_shares(expert_ids, expert_gates, experts):
    shares = expert_gates.astype(jnp.float32)
    shares = shares / jnp.sum(shares, axis=-1, keepdims=True)
    named = expert_ids[..., None] == jnp.arange(experts, dtype=jnp.int32)
    return jnp.sum(jnp.where(named, shares[..., None], 0.0), axis=-2)


def run_expert(rows_in, gate_up, down_proj, weight):
    hidden_width = down_proj.shape[1]
    projected = jnp.dot(rows_in, gate_up[0], preferred_element_type=jnp.float32)
    hidden = (jax.nn.silu(projected[:, :hidden_width]) * projected[:, hidden_width:]).astype(
        jnp.bfloat16
    )
    output = jnp.dot(hidden, down_proj[0], preferred_element_type=jnp.float32)
    return (output * weight).astype(jnp.bfloat16)


MESH = pl.DeviceIdType.MESH


def moe_kernel(
    chips, heads_ref, res_ref, gain_ref, share_ref, gu_hbm, dn_hbm, out_ref,
    attn, stream, gathered, partial, pairbuf, ringbuf, gu, dn, xs, sh, act,
    load_sem, ex_send, ex_recv, ag_send, ag_recv, agp_send, agp_recv, rsp_send, rsp_recv, rs_send, rs_recv,
):
    batches, rows, width = res_ref.shape
    devices = 2 * chips
    kv_heads, part = attn.shape[2], attn.shape[4]
    hidden = dn.shape[0]
    far = chips // 2
    me = lax.axis_index("dev")
    core = me % 2
    mine = me // 2
    odd = mine % 2
    pos = odd * ((mine + 1) // 2) + (1 - odd) * ((chips - mine // 2) % chips)

    def chip_at(place):
        q = (place + 2 * chips) % chips
        upper = q // (far + 1)
        some = (q + chips - 1) // chips
        return some * ((1 - upper) * (2 * q - 1) + upper * 2 * (chips - q))

    partner = mine * 2 + (1 - core)
    ahead = (chip_at(pos + 1) * 2 + core, chip_at(pos - 1) * 2 + core)
    sign = (1, -1)

    def remote(src, dst, send, recv, target):
        return pltpu.make_async_remote_copy(
            src_ref=src, dst_ref=dst, send_sem=send, recv_sem=recv,
            device_id={"dev": target}, device_id_type=MESH,
        )

    def ag_copy(way, dist, batch, origin):
        slot = gathered.at[batch, origin, core]
        return remote(
            slot, slot,
            ag_send.at[way, dist - 1, batch], ag_recv.at[way, dist - 1, batch], ahead[way],
        )

    def pair_copy(batch, origin):
        slot = gathered.at[batch, origin, core]
        return remote(slot, slot, agp_send.at[batch, origin], agp_recv.at[batch, origin], partner)

    def pair_arrival(batch, origin):
        slot = gathered.at[batch, origin, 1 - core]
        return remote(slot, slot, agp_send.at[batch, origin], agp_recv.at[batch, origin], partner)

    def sum_copy(batch, dest):
        return remote(
            partial.at[batch, dest, 1 - core], pairbuf.at[batch, dest],
            rsp_send.at[batch, dest], rsp_recv.at[batch, dest], partner,
        )

    def rs_copy(way, turn, batch, dest):
        return remote(
            partial.at[batch, dest, core], ringbuf.at[way, turn, batch],
            rs_send.at[way, turn, batch], rs_recv.at[way, turn, batch], ahead[way],
        )

    def exchange(batch, target):
        return remote(
            heads_ref.at[batch, target], attn.at[batch, me // kv_heads, me % kv_heads],
            ex_send.at[batch, target], ex_recv.at[batch, me], target,
        )

    def arrival(batch, source):
        slot = attn.at[batch, source // kv_heads, source % kv_heads]
        return remote(slot, slot, ex_send.at[batch, source], ex_recv.at[batch, source], source)

    loads = (
        pltpu.make_async_copy(gu_hbm.at[0], gu, load_sem.at[0]),
        pltpu.make_async_copy(dn_hbm.at[0], dn, load_sem.at[1]),
    )
    for load in loads:
        load.start()

    barrier = pltpu.get_barrier_semaphore()

    @pl.loop(1, devices)
    def _(k):
        target = (me + k) % devices
        pl.semaphore_signal(barrier, inc=1, device_id={"dev": target}, device_id_type=MESH)

    pl.semaphore_wait(barrier, devices - 1)

    for batch in range(batches):

        @pl.loop(1, devices)
        def _(k):
            exchange(batch, (me + k) % devices).start()

    for batch in range(batches):
        attn[batch, me // kv_heads, me % kv_heads] = heads_ref[batch, me]
        gathered[batch, mine, core, :, width:] = share_ref[batch]

        @pl.loop(1, devices)
        def _(k):
            arrival(batch, (me + k) % devices).wait_recv()

        squares = jnp.zeros((rows, 1), jnp.float32)
        for head in range(kv_heads):
            cols = slice(head * part, (head + 1) * part)
            added = attn[batch, :, head].astype(jnp.float32).reshape(rows, part)
            added = added + res_ref[batch, :, cols].astype(jnp.float32)
            stream[batch, :, cols] = added
            squares = squares + jnp.sum(added * added, axis=-1, keepdims=True)
        scale = lax.rsqrt(squares / width + 1e-06)
        gathered[batch, mine, core, :, :width] = (
            stream[batch] * scale * gain_ref[...]
        ).astype(jnp.bfloat16)
        for way in range(2):
            ag_copy(way, 1, batch, mine).start()
        pair_copy(batch, mine).start()
    for load in loads:
        load.wait()

    tile = 256

    def compute(blocks):
        for at, (batch, chip, which) in enumerate(blocks):
            xs[at * rows : (at + 1) * rows, :] = gathered[batch, chip, which, :, :width]
            lanes = gathered[batch, chip, which, :, width:].astype(jnp.float32)
            lane = lax.broadcasted_iota(jnp.int32, lanes.shape, 1)
            mask = (lane == me) | (lane == me + devices)
            share = jnp.sum(jnp.where(mask, lanes, 0.0), axis=-1, keepdims=True)
            sh[at * rows : (at + 1) * rows, :] = jnp.broadcast_to(share, lanes.shape)

        @pl.loop(0, hidden // tile)
        def _(j):
            left = pl.ds(pl.multiple_of(j * tile, tile), tile)
            right = pl.ds(pl.multiple_of(hidden + j * tile, tile), tile)
            gate = jnp.dot(xs[...], gu[:, left], preferred_element_type=jnp.float32)
            up = jnp.dot(xs[...], gu[:, right], preferred_element_type=jnp.float32)
            act[:, left] = (gate / (1.0 + jnp.exp(-gate)) * up).astype(jnp.bfloat16)

        @pl.loop(0, width // (2 * tile))
        def _(j):
            cols = pl.ds(pl.multiple_of(j * 2 * tile, 2 * tile), 2 * tile)
            result = jnp.dot(act[...], dn[:, cols], preferred_element_type=jnp.float32)
            for at, (batch, chip, which) in enumerate(blocks):
                share = sh[at * rows : (at + 1) * rows, :1]
                piece = result[at * rows : (at + 1) * rows]
                partial[batch, chip, which, :, cols] = (piece * share).astype(jnp.bfloat16)

    for batch in range(batches):
        pair_arrival(batch, mine).wait_recv()
    compute([(batch, mine, which) for batch in range(batches) for which in range(2)])
    for batch in range(batches):
        sum_copy(batch, mine).start()

    @pl.loop(0, 2 * (far - 1))
    def _(step):
        dist = step // 2 + 1
        batch = step % 2
        origins = (chip_at(pos - dist), chip_at(pos + dist))
        for way in range(2):
            ag_copy(way, dist, batch, origins[way]).wait_recv()

            @pl.when((dist + 1 < far) | (batch == way))
            def _():
                ag_copy(way, dist + 1, batch, origins[way]).start()

            pair_copy(batch, origins[way]).start()
        for way in range(2):
            pair_arrival(batch, origins[way]).wait_recv()
        compute([(batch, origins[way], which) for way in range(2) for which in range(2)])
        for way in range(2):
            sum_copy(batch, origins[way]).start()

    last = chip_at(pos + far)
    for batch in range(batches):
        ag_copy(batch, far, batch, last).wait_recv()
        pair_copy(batch, last).start()
    for batch in range(batches):
        pair_arrival(batch, last).wait_recv()
    compute([(batch, last, which) for batch in range(batches) for which in range(2)])
    for batch in range(batches):
        sum_copy(batch, last).start()

    def gather_sum(batch, dest):
        return partial[batch, dest, core].astype(jnp.float32) + pairbuf[batch, dest].astype(
            jnp.float32
        )

    for batch in range(batches):
        sum_copy(batch, last).wait_recv()
        partial[batch, last, core] = gather_sum(batch, last).astype(jnp.bfloat16)
        rs_copy(batch, 0, batch, last).start()

    for way in range(2):
        dest = chip_at(pos + sign[way] * (far - 1))
        batch = 1 - way
        sum_copy(batch, dest).wait_recv()
        partial[batch, dest, core] = gather_sum(batch, dest).astype(jnp.bfloat16)
        rs_copy(way, 1, batch, dest).start()
    for way in range(2):
        dest = chip_at(pos + sign[way] * (far - 1))
        batch = way
        sum_copy(batch, dest).wait_recv()
        rs_copy(way, 0, batch, dest).wait_recv()
        partial[batch, dest, core] = (
            gather_sum(batch, dest) + ringbuf[way, 0, batch].astype(jnp.float32)
        ).astype(jnp.bfloat16)
        rs_copy(way, 1, batch, dest).start()

    @pl.loop(0, 2 * (far - 2))
    def _(step):
        turn = step // 2 + 2
        for way in range(2):
            batch = (step + 1 + way) % 2
            dest = chip_at(pos + sign[way] * (far - turn))
            sum_copy(batch, dest).wait_recv()
            rs_copy(way, turn - 1, batch, dest).wait_recv()
            partial[batch, dest, core] = (
                gather_sum(batch, dest) + ringbuf[way, turn - 1, batch].astype(jnp.float32)
            ).astype(jnp.bfloat16)
            rs_copy(way, turn, batch, dest).start()

    for batch in range(batches):
        sum_copy(batch, mine).wait_recv()
    for way in range(2):
        rs_copy(way, far - 1, 1 - way, mine).wait_recv()
    for way in range(2):
        rs_copy(way, far - 1, way, mine).wait_recv()
    for batch in range(batches):
        out_ref[batch] = (
            stream[batch]
            + (
                gather_sum(batch, mine)
                + ringbuf[0, far - 1, batch].astype(jnp.float32)
                + ringbuf[1, far - 1, batch].astype(jnp.float32)
            )
        ).astype(out_ref.dtype)

    @pl.loop(1, devices)
    def _(k):
        for batch in range(batches):
            exchange(batch, (me + k) % devices).wait_send()

    for way in range(2):
        for batch in range(batches):
            ag_copy(way, 1, batch, mine).wait_send()
        ag_copy(way, far, way, mine).wait_send()

        @pl.loop(0, 2 * (far - 2))
        def _(step):
            ag_copy(way, step // 2 + 2, step % 2, mine).wait_send()

        rs_copy(way, 0, way, mine).wait_send()

        @pl.loop(0, 2 * (far - 1))
        def _(step):
            rs_copy(way, step // 2 + 1, step % 2, mine).wait_send()

    @pl.loop(0, 2 * chips)
    def _(step):
        pair_copy(step % 2, step // 2).wait_send()
        sum_copy(step % 2, step // 2).wait_send()


def fits(devices, rows, width, hidden):
    block = 2 * rows * (width + 128) * 2
    needed = 3 * devices * block + 3 * width * hidden * 2 + 8 * rows * width * 4
    return devices % 4 == 0 and 8 <= devices <= 64 and needed < 48 * 1024 * 1024


def share_lanes(weights):
    coarse = lax.reduce_precision(weights, 8, 7)
    fine = lax.reduce_precision(weights - coarse, 8, 7)
    both = jnp.concatenate([coarse, fine], axis=-1)
    gap = 128 - both.shape[-1]
    return jnp.pad(both, ((0, 0), (0, 0), (0, gap))).astype(jnp.bfloat16)


def routed_layer(heads, residual, norm_gain, lanes, gate_up, down_proj, kv_heads):
    batches, rows, width = residual.shape
    devices, span, part = heads.shape[1:]
    hidden = down_proj.shape[1]
    chips = devices // 2
    far = chips // 2
    dma = pltpu.SemaphoreType.DMA
    vmem = pl.BlockSpec(memory_space=pltpu.VMEM)
    anywhere = pl.BlockSpec(memory_space=pl.ANY)
    kind = jnp.bfloat16
    return pl.pallas_call(
        functools.partial(moe_kernel, chips),
        out_shape=jax.ShapeDtypeStruct((batches, rows, width), kind),
        in_specs=[vmem, vmem, vmem, vmem, anywhere, anywhere],
        out_specs=vmem,
        scratch_shapes=[
            pltpu.VMEM((batches, devices // kv_heads, kv_heads, span, part), kind),
            pltpu.VMEM((batches, rows, width), jnp.float32),
            pltpu.VMEM((batches, chips, 2, rows, width + 128), kind),
            pltpu.VMEM((batches, chips, 2, rows, width), kind),
            pltpu.VMEM((batches, chips, rows, width), kind),
            pltpu.VMEM((2, far, batches, rows, width), kind),
            pltpu.VMEM((width, 2 * hidden), kind),
            pltpu.VMEM((hidden, width), kind),
            pltpu.VMEM((4 * rows, width), kind),
            pltpu.VMEM((4 * rows, 128), jnp.float32),
            pltpu.VMEM((4 * rows, hidden), kind),
            dma((2,)),
            dma((batches, devices)), dma((batches, devices)),
            dma((2, far, batches)), dma((2, far, batches)),
            dma((batches, chips)), dma((batches, chips)),
            dma((batches, chips)), dma((batches, chips)),
            dma((2, far, batches)), dma((2, far, batches)),
        ],
        compiler_params=pltpu.CompilerParams(
            collective_id=0, has_side_effects=True, vmem_limit_bytes=56 * 1024 * 1024
        ),
    )(heads, residual, norm_gain.reshape(1, width), lanes, gate_up, down_proj)


def body(queries, keys_values, residual, norm_gain, gate_up, down_proj, expert_ids, expert_gates):
    devices = lax.axis_size("dev")
    me = lax.axis_index("dev")
    model_width = residual.shape[2]
    kv_heads = model_width // queries.shape[3]
    experts = devices * gate_up.shape[0]
    batches, unit, length, feat_width = queries.shape
    positions = length // devices
    weights = dense_shares(expert_ids, expert_gates, experts)
    blended = attend_local(queries, keys_values)
    if batches == 2 and fits(devices, residual.shape[1], model_width, down_proj.shape[1]):
        heads = blended.reshape(batches, devices, positions, feat_width)
        lanes = share_lanes(weights)
        return routed_layer(heads, residual, norm_gain, lanes, gate_up, down_proj, kv_heads)
    weights = lax.all_gather(weights, "dev", axis=1, tiled=True)
    mine = jnp.sum(
        jnp.where(jnp.arange(experts, dtype=jnp.int32) == me, weights, 0.0), axis=-1, keepdims=True
    )
    pieces = []
    for batch_index in range(batches):
        outgoing_rows = blended[batch_index].reshape(1, devices, positions, feat_width)
        arrived_rows = lax.all_to_all(outgoing_rows, "dev", split_axis=1, concat_axis=1, tiled=True)
        attn_rows = to_owners(arrived_rows, kv_heads)
        stream, normed = prepare(attn_rows[0], residual[batch_index], norm_gain)
        rows_in = lax.all_gather(normed, "dev", axis=0, tiled=True)
        partial = run_expert(rows_in, gate_up, down_proj, mine[batch_index])
        summed = lax.psum_scatter(partial, "dev", scatter_dimension=0, tiled=True)
        pieces.append((stream + summed.astype(jnp.float32)).astype(jnp.bfloat16))
    return jnp.stack(pieces, axis=0)


def solution(mesh):
    in_specs = (
        P(None, ("groups", "dev"), None, None),
        P(None, ("groups", "dev"), None, None, None),
        P(None, ("groups", "dev"), None),
        P(),
        P("dev", None, None),
        P("dev", None, None),
        P(None, ("groups", "dev"), None),
        P(None, ("groups", "dev"), None),
    )
    out_specs = P(None, ("groups", "dev"), None)
    return jax.shard_map(body, mesh=mesh, in_specs=in_specs, out_specs=out_specs, check_vma=False)
```

```python
import functools
import math

import jax
import jax.numpy as jnp
from jax import lax
from jax.experimental import pallas as pl
from jax.experimental.pallas import tpu as pltpu
from jax.sharding import PartitionSpec as P


def attend_pair(heads, pair_rows, keys, values):
    length = pair_rows.shape[0]
    context, head_size = keys.shape
    past = context - length
    query = jnp.concatenate(
        [pair_rows[:, head * head_size : (head + 1) * head_size] for head in range(heads)], axis=0
    )
    scores = lax.dot_general(
        query, keys, (((1,), (1,)), ((), ())), preferred_element_type=jnp.float32
    )
    scores = scores * (1.0 / math.sqrt(head_size))
    old, new = scores[:, :past], scores[:, past:]
    row = lax.broadcasted_iota(jnp.int32, new.shape, 0) % length
    col = lax.broadcasted_iota(jnp.int32, new.shape, 1)
    allowed = col <= row
    new = jnp.where(allowed, new, -1e30)
    highest = jnp.maximum(
        jnp.max(old, axis=-1, keepdims=True), jnp.max(new, axis=-1, keepdims=True)
    )
    old = jnp.exp(old - highest)
    new = jnp.where(allowed, jnp.exp(new - highest), 0.0)
    totals = jnp.sum(old, axis=-1, keepdims=True) + jnp.sum(new, axis=-1, keepdims=True)
    share = 1.0 / totals
    blended = jnp.dot(
        (old * share).astype(jnp.bfloat16), values[:past],
        preferred_element_type=jnp.float32,
    ) + jnp.dot(
        (new * share).astype(jnp.bfloat16), values[past:],
        preferred_element_type=jnp.float32,
    )
    return blended


def attend_kernel(heads, q_ref, kv_ref, out_ref):
    length = q_ref.shape[1]
    head_size = kv_ref.shape[4]
    blended = attend_pair(heads, q_ref[0], kv_ref[0, 0, 0], kv_ref[0, 0, 1])
    for head in range(heads):
        out_ref[0, :, head * head_size : (head + 1) * head_size] = blended[
            head * length : (head + 1) * length
        ].astype(jnp.bfloat16)


def attend_local(queries, keys_values):
    batches, unit, length, feat_width = queries.shape
    context, head_size = keys_values.shape[3:]
    heads = 2
    wide = heads * head_size
    return pl.pallas_call(
        functools.partial(attend_kernel, heads),
        grid=(batches, feat_width // wide),
        out_shape=jax.ShapeDtypeStruct((batches, length, feat_width), jnp.bfloat16),
        in_specs=[
            pl.BlockSpec((1, length, wide), lambda b, h: (b, 0, h)),
            pl.BlockSpec((1, 1, 2, context, head_size), lambda b, h: (b, 0, 0, 0, 0)),
        ],
        out_specs=pl.BlockSpec((1, length, wide), lambda b, h: (b, 0, h)),
        compiler_params=pltpu.CompilerParams(vmem_limit_bytes=40 * 1024 * 1024),
    )(queries.reshape(batches, length, feat_width), keys_values)


def to_owners(exchanged, kv_heads):
    batches, sources, positions, feat_width = exchanged.shape
    grouped = exchanged.reshape(batches, sources // kv_heads, kv_heads, positions, feat_width)
    grouped = jnp.transpose(grouped, (0, 1, 3, 2, 4))
    return grouped.reshape(batches, sources // kv_heads * positions, kv_heads * feat_width)


def prepare(attn_rows, residual, norm_gain):
    stream = residual.astype(jnp.float32) + attn_rows.astype(jnp.float32)
    meansq = jnp.mean(stream * stream, axis=-1, keepdims=True)
    normed = (stream * lax.rsqrt(meansq + 1e-06) * norm_gain).astype(jnp.bfloat16)
    return stream, normed


def dense_shares(expert_ids, expert_gates, experts):
    shares = expert_gates.astype(jnp.float32)
    shares = shares / jnp.sum(shares, axis=-1, keepdims=True)
    named = expert_ids[..., None] == jnp.arange(experts, dtype=jnp.int32)
    return jnp.sum(jnp.where(named, shares[..., None], 0.0), axis=-2)


def run_expert(rows_in, gate_up, down_proj, weight):
    hidden_width = down_proj.shape[1]
    projected = jnp.dot(rows_in, gate_up[0], preferred_element_type=jnp.float32)
    hidden = (jax.nn.silu(projected[:, :hidden_width]) * projected[:, hidden_width:]).astype(
        jnp.bfloat16
    )
    output = jnp.dot(hidden, down_proj[0], preferred_element_type=jnp.float32)
    return (output * weight).astype(jnp.bfloat16)


MESH = pl.DeviceIdType.MESH


def moe_kernel(
    chips, q_ref, kv_ref, res_ref, gain_ref, share_ref, gu_hbm, dn_hbm, out_ref,
    heads_ref, attn, stream, gathered, partial, pairbuf, ringbuf, gu, dn, xs, sh, act,
    load_sem, ex_send, ex_recv, ag_send, ag_recv, agp_send, agp_recv, rsp_send, rsp_recv, rs_send, rs_recv,
):
    batches, rows, width = res_ref.shape
    devices = 2 * chips
    kv_heads, part = attn.shape[2], attn.shape[4]
    hidden = dn.shape[0]
    far = chips // 2
    me = lax.axis_index("dev")
    core = me % 2
    mine = me // 2
    odd = mine % 2
    pos = odd * ((mine + 1) // 2) + (1 - odd) * ((chips - mine // 2) % chips)

    def chip_at(place):
        q = (place + 2 * chips) % chips
        upper = q // (far + 1)
        some = (q + chips - 1) // chips
        return some * ((1 - upper) * (2 * q - 1) + upper * 2 * (chips - q))

    partner = mine * 2 + (1 - core)
    ahead = (chip_at(pos + 1) * 2 + core, chip_at(pos - 1) * 2 + core)
    sign = (1, -1)

    def remote(src, dst, send, recv, target):
        return pltpu.make_async_remote_copy(
            src_ref=src, dst_ref=dst, send_sem=send, recv_sem=recv,
            device_id={"dev": target}, device_id_type=MESH,
        )

    def ag_copy(way, dist, batch, origin):
        slot = gathered.at[batch, origin, core]
        return remote(
            slot, slot,
            ag_send.at[way, dist - 1, batch], ag_recv.at[way, dist - 1, batch], ahead[way],
        )

    def pair_copy(batch, origin):
        slot = gathered.at[batch, origin, core]
        return remote(slot, slot, agp_send.at[batch, origin], agp_recv.at[batch, origin], partner)

    def pair_arrival(batch, origin):
        slot = gathered.at[batch, origin, 1 - core]
        return remote(slot, slot, agp_send.at[batch, origin], agp_recv.at[batch, origin], partner)

    def sum_copy(batch, dest):
        return remote(
            partial.at[batch, dest, 1 - core], pairbuf.at[batch, dest],
            rsp_send.at[batch, dest], rsp_recv.at[batch, dest], partner,
        )

    def rs_copy(way, turn, batch, dest):
        return remote(
            partial.at[batch, dest, core], ringbuf.at[way, turn, batch],
            rs_send.at[way, turn, batch], rs_recv.at[way, turn, batch], ahead[way],
        )

    def exchange(batch, target):
        return remote(
            heads_ref.at[batch, target], attn.at[batch, me // kv_heads, me % kv_heads],
            ex_send.at[batch, target], ex_recv.at[batch, me], target,
        )

    def arrival(batch, source):
        slot = attn.at[batch, source // kv_heads, source % kv_heads]
        return remote(slot, slot, ex_send.at[batch, source], ex_recv.at[batch, source], source)

    loads = (
        pltpu.make_async_copy(gu_hbm.at[0], gu, load_sem.at[0]),
        pltpu.make_async_copy(dn_hbm.at[0], dn, load_sem.at[1]),
    )
    for load in loads:
        load.start()

    barrier = pltpu.get_barrier_semaphore()

    @pl.loop(1, devices)
    def _(k):
        target = (me + k) % devices
        pl.semaphore_signal(barrier, inc=1, device_id={"dev": target}, device_id_type=MESH)

    head_size = kv_ref.shape[3]
    for batch in range(batches):

        @pl.loop(0, part // (2 * head_size))
        def _(h):
            cols = pl.ds(pl.multiple_of(h * 2 * head_size, 2 * head_size), 2 * head_size)
            blended = attend_pair(2, q_ref[batch, :, cols], kv_ref[batch, 0], kv_ref[batch, 1])
            length = q_ref.shape[1]
            for head in range(2):
                at = pl.ds(pl.multiple_of((h * 2 + head) * head_size, head_size), head_size)
                piece = blended[head * length : (head + 1) * length]
                heads_ref[batch, :, :, at] = piece.reshape(
                    devices, length // devices, head_size
                ).astype(jnp.bfloat16)

        if batch == 0:
            pl.semaphore_wait(barrier, devices - 1)

        @pl.loop(1, devices)
        def _(k):
            exchange(batch, (me + k) % devices).start()

    for batch in range(batches):
        attn[batch, me // kv_heads, me % kv_heads] = heads_ref[batch, me]
        gathered[batch, mine, core, :, width:] = share_ref[batch]

        @pl.loop(1, devices)
        def _(k):
            arrival(batch, (me + k) % devices).wait_recv()

        squares = jnp.zeros((rows, 1), jnp.float32)
        for head in range(kv_heads):
            cols = slice(head * part, (head + 1) * part)
            added = attn[batch, :, head].astype(jnp.float32).reshape(rows, part)
            added = added + res_ref[batch, :, cols].astype(jnp.float32)
            stream[batch, :, cols] = added
            squares = squares + jnp.sum(added * added, axis=-1, keepdims=True)
        scale = lax.rsqrt(squares / width + 1e-06)
        gathered[batch, mine, core, :, :width] = (
            stream[batch] * scale * gain_ref[...]
        ).astype(jnp.bfloat16)
        for way in range(2):
            ag_copy(way, 1, batch, mine).start()
        pair_copy(batch, mine).start()
    for load in loads:
        load.wait()

    tile = 256

    def compute(blocks):
        for at, (batch, chip, which) in enumerate(blocks):
            xs[at * rows : (at + 1) * rows, :] = gathered[batch, chip, which, :, :width]
            lanes = gathered[batch, chip, which, :, width:].astype(jnp.float32)
            lane = lax.broadcasted_iota(jnp.int32, lanes.shape, 1)
            mask = (lane == me) | (lane == me + devices)
            share = jnp.sum(jnp.where(mask, lanes, 0.0), axis=-1, keepdims=True)
            sh[at * rows : (at + 1) * rows, :] = jnp.broadcast_to(share, lanes.shape)

        @pl.loop(0, hidden // tile)
        def _(j):
            left = pl.ds(pl.multiple_of(j * tile, tile), tile)
            right = pl.ds(pl.multiple_of(hidden + j * tile, tile), tile)
            gate = jnp.dot(xs[...], gu[:, left], preferred_element_type=jnp.float32)
            up = jnp.dot(xs[...], gu[:, right], preferred_element_type=jnp.float32)
            act[:, left] = (gate / (1.0 + jnp.exp(-gate)) * up).astype(jnp.bfloat16)

        @pl.loop(0, width // (2 * tile))
        def _(j):
            cols = pl.ds(pl.multiple_of(j * 2 * tile, 2 * tile), 2 * tile)
            result = jnp.dot(act[...], dn[:, cols], preferred_element_type=jnp.float32)
            for at, (batch, chip, which) in enumerate(blocks):
                share = sh[at * rows : (at + 1) * rows, :1]
                piece = result[at * rows : (at + 1) * rows]
                partial[batch, chip, which, :, cols] = (piece * share).astype(jnp.bfloat16)

    for batch in range(batches):
        pair_arrival(batch, mine).wait_recv()
    compute([(batch, mine, which) for batch in range(batches) for which in range(2)])
    for batch in range(batches):
        sum_copy(batch, mine).start()

    @pl.loop(0, 2 * (far - 1))
    def _(step):
        dist = step // 2 + 1
        batch = step % 2
        origins = (chip_at(pos - dist), chip_at(pos + dist))
        for way in range(2):
            ag_copy(way, dist, batch, origins[way]).wait_recv()

            @pl.when((dist + 1 < far) | (batch == way))
            def _():
                ag_copy(way, dist + 1, batch, origins[way]).start()

            pair_copy(batch, origins[way]).start()
        for way in range(2):
            pair_arrival(batch, origins[way]).wait_recv()
        compute([(batch, origins[way], which) for way in range(2) for which in range(2)])
        for way in range(2):
            sum_copy(batch, origins[way]).start()

    last = chip_at(pos + far)
    for batch in range(batches):
        ag_copy(batch, far, batch, last).wait_recv()
        pair_copy(batch, last).start()
    for batch in range(batches):
        pair_arrival(batch, last).wait_recv()
    compute([(batch, last, which) for batch in range(batches) for which in range(2)])
    for batch in range(batches):
        sum_copy(batch, last).start()

    def gather_sum(batch, dest):
        return partial[batch, dest, core].astype(jnp.float32) + pairbuf[batch, dest].astype(
            jnp.float32
        )

    for batch in range(batches):
        sum_copy(batch, last).wait_recv()
        partial[batch, last, core] = gather_sum(batch, last).astype(jnp.bfloat16)
        rs_copy(batch, 0, batch, last).start()

    for way in range(2):
        dest = chip_at(pos + sign[way] * (far - 1))
        batch = 1 - way
        sum_copy(batch, dest).wait_recv()
        partial[batch, dest, core] = gather_sum(batch, dest).astype(jnp.bfloat16)
        rs_copy(way, 1, batch, dest).start()
    for way in range(2):
        dest = chip_at(pos + sign[way] * (far - 1))
        batch = way
        sum_copy(batch, dest).wait_recv()
        rs_copy(way, 0, batch, dest).wait_recv()
        partial[batch, dest, core] = (
            gather_sum(batch, dest) + ringbuf[way, 0, batch].astype(jnp.float32)
        ).astype(jnp.bfloat16)
        rs_copy(way, 1, batch, dest).start()

    @pl.loop(0, 2 * (far - 2))
    def _(step):
        turn = step // 2 + 2
        for way in range(2):
            batch = (step + 1 + way) % 2
            dest = chip_at(pos + sign[way] * (far - turn))
            sum_copy(batch, dest).wait_recv()
            rs_copy(way, turn - 1, batch, dest).wait_recv()
            partial[batch, dest, core] = (
                gather_sum(batch, dest) + ringbuf[way, turn - 1, batch].astype(jnp.float32)
            ).astype(jnp.bfloat16)
            rs_copy(way, turn, batch, dest).start()

    for batch in range(batches):
        sum_copy(batch, mine).wait_recv()
    for way in range(2):
        rs_copy(way, far - 1, 1 - way, mine).wait_recv()
    for way in range(2):
        rs_copy(way, far - 1, way, mine).wait_recv()
    for batch in range(batches):
        out_ref[batch] = (
            stream[batch]
            + (
                gather_sum(batch, mine)
                + ringbuf[0, far - 1, batch].astype(jnp.float32)
                + ringbuf[1, far - 1, batch].astype(jnp.float32)
            )
        ).astype(out_ref.dtype)

    @pl.loop(1, devices)
    def _(k):
        for batch in range(batches):
            exchange(batch, (me + k) % devices).wait_send()

    for way in range(2):
        for batch in range(batches):
            ag_copy(way, 1, batch, mine).wait_send()
        ag_copy(way, far, way, mine).wait_send()

        @pl.loop(0, 2 * (far - 2))
        def _(step):
            ag_copy(way, step // 2 + 2, step % 2, mine).wait_send()

        rs_copy(way, 0, way, mine).wait_send()

        @pl.loop(0, 2 * (far - 1))
        def _(step):
            rs_copy(way, step // 2 + 1, step % 2, mine).wait_send()

    @pl.loop(0, 2 * chips)
    def _(step):
        pair_copy(step % 2, step // 2).wait_send()
        sum_copy(step % 2, step // 2).wait_send()


def fits(devices, rows, width, hidden):
    block = 2 * rows * (width + 128) * 2
    needed = 3 * devices * block + 3 * width * hidden * 2 + 8 * rows * width * 4
    return devices % 4 == 0 and 8 <= devices <= 64 and needed < 48 * 1024 * 1024


def share_lanes(weights):
    coarse = lax.reduce_precision(weights, 8, 7)
    fine = lax.reduce_precision(weights - coarse, 8, 7)
    both = jnp.concatenate([coarse, fine], axis=-1)
    gap = 128 - both.shape[-1]
    return jnp.pad(both, ((0, 0), (0, 0), (0, gap))).astype(jnp.bfloat16)


def routed_layer(queries, keys_values, residual, norm_gain, lanes, gate_up, down_proj, kv_heads, devices):
    batches, rows, width = residual.shape
    length, part = queries.shape[1:]
    span = length // devices
    hidden = down_proj.shape[1]
    chips = devices // 2
    far = chips // 2
    dma = pltpu.SemaphoreType.DMA
    vmem = pl.BlockSpec(memory_space=pltpu.VMEM)
    anywhere = pl.BlockSpec(memory_space=pl.ANY)
    kind = jnp.bfloat16
    return pl.pallas_call(
        functools.partial(moe_kernel, chips),
        out_shape=jax.ShapeDtypeStruct((batches, rows, width), kind),
        in_specs=[vmem, vmem, vmem, vmem, vmem, anywhere, anywhere],
        out_specs=vmem,
        scratch_shapes=[
            pltpu.VMEM((batches, devices, span, part), kind),
            pltpu.VMEM((batches, devices // kv_heads, kv_heads, span, part), kind),
            pltpu.VMEM((batches, rows, width), jnp.float32),
            pltpu.VMEM((batches, chips, 2, rows, width + 128), kind),
            pltpu.VMEM((batches, chips, 2, rows, width), kind),
            pltpu.VMEM((batches, chips, rows, width), kind),
            pltpu.VMEM((2, far, batches, rows, width), kind),
            pltpu.VMEM((width, 2 * hidden), kind),
            pltpu.VMEM((hidden, width), kind),
            pltpu.VMEM((4 * rows, width), kind),
            pltpu.VMEM((4 * rows, 128), jnp.float32),
            pltpu.VMEM((4 * rows, hidden), kind),
            dma((2,)),
            dma((batches, devices)), dma((batches, devices)),
            dma((2, far, batches)), dma((2, far, batches)),
            dma((batches, chips)), dma((batches, chips)),
            dma((batches, chips)), dma((batches, chips)),
            dma((2, far, batches)), dma((2, far, batches)),
        ],
        compiler_params=pltpu.CompilerParams(
            collective_id=0, has_side_effects=True, vmem_limit_bytes=56 * 1024 * 1024
        ),
    )(queries, keys_values, residual, norm_gain.reshape(1, width), lanes, gate_up, down_proj)


def body(queries, keys_values, residual, norm_gain, gate_up, down_proj, expert_ids, expert_gates):
    devices = lax.axis_size("dev")
    me = lax.axis_index("dev")
    model_width = residual.shape[2]
    kv_heads = model_width // queries.shape[3]
    experts = devices * gate_up.shape[0]
    batches, unit, length, feat_width = queries.shape
    positions = length // devices
    weights = dense_shares(expert_ids, expert_gates, experts)
    if batches == 2 and fits(devices, residual.shape[1], model_width, down_proj.shape[1]):
        lanes = share_lanes(weights)
        return routed_layer(
            queries[:, 0], keys_values[:, 0], residual, norm_gain, lanes, gate_up, down_proj,
            kv_heads, devices,
        )
    blended = attend_local(queries, keys_values)
    weights = lax.all_gather(weights, "dev", axis=1, tiled=True)
    mine = jnp.sum(
        jnp.where(jnp.arange(experts, dtype=jnp.int32) == me, weights, 0.0), axis=-1, keepdims=True
    )
    pieces = []
    for batch_index in range(batches):
        outgoing_rows = blended[batch_index].reshape(1, devices, positions, feat_width)
        arrived_rows = lax.all_to_all(outgoing_rows, "dev", split_axis=1, concat_axis=1, tiled=True)
        attn_rows = to_owners(arrived_rows, kv_heads)
        stream, normed = prepare(attn_rows[0], residual[batch_index], norm_gain)
        rows_in = lax.all_gather(normed, "dev", axis=0, tiled=True)
        partial = run_expert(rows_in, gate_up, down_proj, mine[batch_index])
        summed = lax.psum_scatter(partial, "dev", scatter_dimension=0, tiled=True)
        pieces.append((stream + summed.astype(jnp.float32)).astype(jnp.bfloat16))
    return jnp.stack(pieces, axis=0)


def solution(mesh):
    in_specs = (
        P(None, ("groups", "dev"), None, None),
        P(None, ("groups", "dev"), None, None, None),
        P(None, ("groups", "dev"), None),
        P(),
        P("dev", None, None),
        P("dev", None, None),
        P(None, ("groups", "dev"), None),
        P(None, ("groups", "dev"), None),
    )
    out_specs = P(None, ("groups", "dev"), None)
    return jax.shard_map(body, mesh=mesh, in_specs=in_specs, out_specs=out_specs, check_vma=False)
```
